128 devices in a mesh: tm: 2 (over z_hi), lon: 16 (over y, x), head: 4 (over z_lo, core).
Axes of the slice: x: 4, y: 4, z: 4 (z_hi: 2, z_lo: 2; z = z_hi * 2 + z_lo), core: 2. Of those that a mesh axis runs over, the one named last changes fastest.
Arguments:
- query_rows: bfloat16 [8, 8, 128, 5120], P('tm', None, 'lon', 'head'), may hold values from -16 to 16
- key_rows: bfloat16 [8, 8, 128, 5120], P('tm', None, 'lon', 'head'), may hold values from -16 to 16
- value_rows: bfloat16 [8, 8, 128, 5120], P('tm', None, 'lon', 'head'), may hold values from -6 to 6
- out_grad: bfloat16 [8, 8, 128, 5120], P('tm', None, 'lon', 'head'), may hold values from -6 to 6
- window_offsets: int32 [2, 2, 32], P('tm', None, 'lon'), may hold values from -1 to 1
Outputs:
- attended: bfloat16 [8, 8, 128, 5120], P('tm', None, 'lon', 'head')
- query_grad: bfloat16 [8, 8, 128, 5120], P('tm', None, 'lon', 'head')
- key_grad: bfloat16 [8, 8, 128, 5120], P('tm', None, 'lon', 'head')
- value_grad: bfloat16 [8, 8, 128, 5120], P('tm', None, 'lon', 'head')
The draws below stay inside these ranges and needn't reach their ends.
All inputs are finite; a program needn't handle non-finite values.
Results may differ from the reference program's by a relative error of at most 0.013.
The reference program's roundings to bfloat16 on the way (of `probs` and `dscores`) count: a program that leaves them out, or rounds other values in their place, can miss the bound.
Values may be sent and summed in bfloat16 or wider, within the bound.
A program may use at most 128 MiB of HBM per device.

```python
import math
import jax
import jax.numpy as jnp
from jax import lax

HEADS = 40
HD = 128
TILE = 4
LAT = 8
FRAMES = 8
LON = 128


def draw_query_rows(key, part):
    shape = (FRAMES, LAT, LON, HEADS * HD)
    noise_key = jax.random.fold_in(key, 1)
    values = jnp.clip(jax.random.normal(noise_key, shape, jnp.float32), -6.0, 6.0)
    return values.astype(jnp.bfloat16)


def draw_key_rows(key, part):
    shape = (FRAMES, LAT, LON, HEADS * HD)
    noise_key = jax.random.fold_in(key, 2)
    values = jnp.clip(jax.random.normal(noise_key, shape, jnp.float32), -6.0, 6.0)
    return values.astype(jnp.bfloat16)


def touch_ends(entries, own_key, least, high):
    dims = entries.shape
    place = [jax.random.randint(jax.random.fold_in(own_key, axis), (), 0, dims[axis]) for axis in range(len(dims))]
    entries = entries.at[tuple(place)].set(least)
    longest = dims.index(max(dims))
    place[longest] = (place[longest] + 1) % dims[longest]
    return entries.at[tuple(place)].set(high)


def level_of(stream_key, extent, pieces, least, high):
    factor_of = 1.0
    for axis_at, parts in pieces:
        draws = jax.random.uniform(jax.random.fold_in(jax.random.fold_in(stream_key, 6), axis_at), (parts,), jnp.float32, least / len(pieces), high / len(pieces))
        factor_of = factor_of * jnp.repeat(jnp.exp(draws), extent[axis_at] // parts).reshape((-1,) + (1,) * (len(extent) - 1 - axis_at))
    return factor_of


def noise(rng, extent, spread, bound, shards=(), held_as=jnp.bfloat16):
    entries = spread * jax.random.normal(rng, extent, jnp.float32)
    if shards:
        entries = entries * level_of(rng, extent, shards, -0.22, 0.18)
    return jnp.clip(entries, -bound, bound).astype(held_as)


def setup_inputs(seed: int = 0) -> dict:
    seeds = jax.random.split(jax.random.key(seed), 6)
    return {
        "query_rows": draw_query_rows(jax.random.fold_in(seeds[5], 71), 0),
        "key_rows": draw_key_rows(jax.random.fold_in(seeds[5], 71), 0),
        "value_rows": noise(seeds[2], (FRAMES, LAT, LON, HEADS * HD), 1.0, 6.0, ((0, 2), (2, 16), (3, 4))),
        "out_grad": noise(seeds[3], (FRAMES, LAT, LON, HEADS * HD), 1.0, 6.0, ((0, 2), (2, 16), (3, 4))),
        "window_offsets": touch_ends(jax.random.randint(seeds[4], (FRAMES // TILE, LAT // TILE, LON // TILE), -1, 2), jax.random.fold_in(seeds[4], 1), -1, 1).astype(jnp.int32),
    }


def reference(query_rows, key_rows, value_rows, out_grad, window_offsets):
    scale = 1.0 / math.sqrt(HD)
    frame_tiles = FRAMES // TILE
    lat_tiles = LAT // TILE
    lon_tiles = LON // TILE
    block_count = frame_tiles * lat_tiles * lon_tiles
    span = jnp.arange(3 * TILE).astype(jnp.int32)
    span_tile = (span // TILE - 1).astype(jnp.int32)
    cube = (3 * TILE, 3 * TILE, 3 * TILE)

    def to_heads(array):
        return array.reshape(FRAMES, LAT, LON, HEADS, HD).transpose(3, 0, 1, 2, 4)

    def per_head(inputs):
        query_head, key_head, value_head, grad_head = inputs

        def block(carry, index):
            key_acc, value_acc = carry
            frame_tile = (index // (lat_tiles * lon_tiles)).astype(jnp.int32)
            lat_tile = (index // lon_tiles % lat_tiles).astype(jnp.int32)
            lon_tile = (index % lon_tiles).astype(jnp.int32)
            offset = window_offsets[frame_tile, lat_tile, lon_tile].astype(jnp.int32)
            frame_index = jnp.clip(frame_tile * TILE - TILE + span, 0, FRAMES - 1).astype(jnp.int32)
            lat_index = jnp.clip(lat_tile * TILE - TILE + span, 0, LAT - 1).astype(jnp.int32)
            lon_index = (((lon_tile + offset - 1) * TILE + span) % LON).astype(jnp.int32)
            frame_ok = (frame_tile + span_tile >= 0) & (frame_tile + span_tile < frame_tiles)
            lat_ok = (lat_tile + span_tile >= 0) & (lat_tile + span_tile < lat_tiles)
            allowed = jnp.broadcast_to(frame_ok[:, None, None] & lat_ok[None, :, None], cube).reshape(-1)
            anchor = jnp.int32(0)
            corner = ((frame_tile * TILE).astype(jnp.int32), (lat_tile * TILE).astype(jnp.int32), (lon_tile * TILE).astype(jnp.int32), anchor)
            query_full = lax.dynamic_slice(query_head, corner, (TILE, TILE, TILE, HD)).astype(jnp.float32).reshape(-1, HD)
            grad_full = lax.dynamic_slice(grad_head, corner, (TILE, TILE, TILE, HD)).astype(jnp.float32).reshape(-1, HD)
            where = (frame_index[:, None, None], lat_index[None, :, None], lon_index[None, None, :])
            key_full = key_head[where].astype(jnp.float32).reshape(-1, HD)
            value_full = value_head[where].astype(jnp.float32).reshape(-1, HD)
            scores = jnp.dot(query_full, key_full.T, precision=lax.Precision.HIGHEST) * scale
            peak = lax.optimization_barrier(jnp.max(jnp.where(allowed[None, :], scores, -jnp.inf), axis=1, keepdims=True))
            expo = jnp.exp(jnp.where(allowed[None, :], scores - peak, -jnp.inf))
            probs = (expo / lax.optimization_barrier(jnp.sum(expo, axis=1, keepdims=True))).astype(jnp.bfloat16)
            probs_full = lax.optimization_barrier(probs).astype(jnp.float32)
            attended = jnp.dot(probs_full, value_full, precision=lax.Precision.HIGHEST).astype(jnp.bfloat16)
            attended_full = lax.optimization_barrier(attended).astype(jnp.float32)
            delta = lax.optimization_barrier(jnp.sum(grad_full * attended_full, axis=1, keepdims=True))
            dprobs = jnp.dot(grad_full, value_full.T, precision=lax.Precision.HIGHEST)
            dscores = (probs_full * (dprobs - delta)).astype(jnp.bfloat16)
            dscores_full = lax.optimization_barrier(dscores).astype(jnp.float32)
            query_grad = (jnp.dot(dscores_full, key_full, precision=lax.Precision.HIGHEST) * scale).astype(jnp.bfloat16)
            key_part = jnp.dot(dscores_full.T, query_full, precision=lax.Precision.HIGHEST) * scale
            value_part = jnp.dot(probs_full.T, grad_full, precision=lax.Precision.HIGHEST)
            key_acc = key_acc.at[where].add(key_part.reshape(cube + (HD,)))
            value_acc = value_acc.at[where].add(value_part.reshape(cube + (HD,)))
            return ((key_acc, value_acc), (attended, query_grad))
        zero_acc = jnp.zeros((FRAMES, LAT, LON, HD), jnp.float32)
        indices = jnp.arange(block_count).astype(jnp.int32)
        (key_acc, value_acc), (attended, query_grad) = lax.scan(block, (zero_acc, zero_acc), indices)

        def assemble(blocks):
            shaped = blocks.reshape(frame_tiles, lat_tiles, lon_tiles, TILE, TILE, TILE, HD)
            return shaped.transpose(0, 3, 1, 4, 2, 5, 6).reshape(FRAMES, LAT, LON, HD)
        return (assemble(attended), assemble(query_grad), key_acc.astype(jnp.bfloat16), value_acc.astype(jnp.bfloat16))
    results = lax.map(per_head, (to_heads(query_rows), to_heads(key_rows), to_heads(value_rows), to_heads(out_grad)))

    def from_heads(array):
        return array.transpose(1, 2, 3, 0, 4).reshape(FRAMES, LAT, LON, HEADS * HD)
    return (from_heads(results[0]), from_heads(results[1]), from_heads(results[2]), from_heads(results[3]))
```

```python
import math

import jax
import jax.numpy as jnp
from jax import lax
from jax.experimental import pallas as pl
from jax.experimental.pallas import tpu as pltpu
from jax.sharding import PartitionSpec as P

HD = 128
TILE = 4
MESH = pl.DeviceIdType.MESH
SCALE = 1.0 / math.sqrt(HD)
EXP_SCALE = SCALE / math.log(2.0)
FAR = -1e30
BF16 = jnp.bfloat16
F32 = jnp.float32
CONTRACT_LAST = (((1,), (1,)), ((), ()))
CONTRACT_FIRST = (((0,), (0,)), ((), ()))


def kernel(
    heads, rows, lats, lons,
    q_in, k_in, v_in, g_in, off_in,
    o_out, dq_out, dk_out, dv_out,
    qb, gb, kv, offs, bias, scores, ob, dqb, back_send, back_recv, own_grad, grad_out,
    load_sem, off_sem, zf_send, zf_recv, xo_send, xo_recv, xp_send, xp_recv,
    xb_send, xb_recv, zb_send, zb_recv, out_sem,
):
    me = lax.axis_index("tm")
    lon = lax.axis_index("lon")
    count = lax.axis_size("lon")
    peer = 1 - me
    sides = (lax.rem(lon + 1, count), lax.rem(lon + count - 1, count))
    full = 2 * rows
    args = (k_in, v_in, q_in, g_in)
    outs = (o_out, dq_out, dk_out, dv_out)

    def columns(owner, j):
        return pl.ds(pl.multiple_of((owner * heads + j) * HD, HD), HD)

    def half(owner):
        return pl.ds(pl.multiple_of(owner * rows, rows), rows)

    def slot(t, j):
        part = kv.at[1, j, t] if t < 2 else (qb.at[j] if t == 2 else gb.at[j])
        return part.at[half(me)]

    def load(t, j):
        return pltpu.make_async_copy(args[t].at[:, columns(me, j)], slot(t, j), load_sem.at[t, j])

    def z_forward(t, j):
        return pltpu.make_async_remote_copy(
            args[t].at[:, columns(peer, j)], slot(t, j), zf_send.at[t, j], zf_recv.at[t, j],
            device_id={"tm": peer}, device_id_type=MESH)

    def x_own(d, t, j):
        return pltpu.make_async_remote_copy(
            args[t].at[:, columns(me, j)], kv.at[2 * d, j, t, half(me)],
            xo_send.at[d, t, j], xo_recv.at[d, t, j],
            device_id={"lon": sides[d]}, device_id_type=MESH)

    def x_peer(d, t, j):
        return pltpu.make_async_remote_copy(
            kv.at[1, j, t, half(peer)], kv.at[2 * d, j, t, half(peer)],
            xp_send.at[d, t, j], xp_recv.at[d, t, j],
            device_id={"lon": sides[d]}, device_id_type=MESH)

    def x_back(d, t, j):
        return pltpu.make_async_remote_copy(
            back_send.at[d, j, t], back_recv.at[d, j, t], xb_send.at[d, t, j], xb_recv.at[d, t, j],
            device_id={"lon": sides[d]}, device_id_type=MESH)

    def result(t, j):
        return (ob.at[j], dqb.at[j], grad_out.at[j, 0], grad_out.at[j, 1])[t]

    def z_back(t, j):
        return pltpu.make_async_remote_copy(
            result(t, j).at[half(peer)], outs[t].at[:, columns(me, j)],
            zb_send.at[t, j], zb_recv.at[t, j],
            device_id={"tm": peer}, device_id_type=MESH)

    def store(t, j):
        return pltpu.make_async_copy(
            result(t, j).at[half(me)], outs[t].at[:, columns(me, j)], out_sem.at[t, j])

    off_load = pltpu.make_async_copy(off_in, offs.at[me], off_sem.at[0])
    off_send = pltpu.make_async_remote_copy(
        off_in, offs.at[me], off_sem.at[1], off_sem.at[2],
        device_id={"tm": peer}, device_id_type=MESH)

    def each(body):
        lax.fori_loop(0, heads, lambda j, c: (body(j), c)[1], 0)

    barrier = pltpu.get_barrier_semaphore()
    pl.semaphore_signal(barrier, inc=1, device_id={"tm": peer}, device_id_type=MESH)
    for side in sides:
        pl.semaphore_signal(barrier, inc=1, device_id={"lon": side}, device_id_type=MESH)
    pl.semaphore_wait(barrier, 3)

    off_send.start()
    off_load.start()

    def begin(j):
        for t in range(2):
            z_forward(t, j).start()
            for d in range(2):
                x_own(d, t, j).start()
        for t in range(4):
            load(t, j).start()

    each(begin)

    def begin_queries(j):
        for t in range(2, 4):
            z_forward(t, j).start()

    each(begin_queries)

    off_load.wait()
    off_send.wait()
    query = lax.broadcasted_iota(jnp.int32, (8, full), 1)
    sub = lax.broadcasted_iota(jnp.int32, (8, full), 0)
    q_frame = query // rows
    q_lat = (query // (lons * TILE)) % 2
    q_lon = (query // TILE) % 2
    centre = q_lon
    for f in range(2):
        for a in range(2):
            for b in range(2):
                value = offs[f, a : a + 1, b : b + 1]
                hit = (q_frame == f) & (q_lat == a) & (q_lon == b)
                centre = centre + jnp.where(hit, value, 0)
    for b in range(3):
        gap = sub // TILE + (2 * b - 2) - centre
        bias[b] = jnp.where(jnp.abs(gap) <= 1, 0.0, FAR).astype(F32)

    def forward_peer(j):
        for t in range(2):
            z_forward(t, j).wait_recv()
            for d in range(2):
                x_peer(d, t, j).start()

    each(forward_peer)

    groups = full // 8

    def head(j):
        for t in range(4):
            load(t, j).wait()
        for t in range(2, 4):
            z_forward(t, j).wait_recv()
        for d in range(2):
            for t in range(2):
                x_own(d, t, j).wait_recv()
                x_peer(d, t, j).wait_recv()
        q = qb[j]
        g = gb[j]
        peak = None
        for b in range(3):
            s = lax.dot_general(kv[b, j, 0], q, CONTRACT_LAST, preferred_element_type=F32)
            s = s.reshape(groups, 8, full) + bias[b]
            scores[b] = s.reshape(full, full)
            top = jnp.max(s, axis=0)
            peak = top if peak is None else jnp.maximum(peak, top)
        peak = jnp.max(peak, axis=0, keepdims=True)
        total = jnp.zeros((8, full), F32)
        out_t = jnp.zeros((HD, full), F32)
        for b in range(3):
            p = jnp.exp2((scores[b] - peak) * EXP_SCALE)
            scores[b] = p
            total = total + jnp.sum(p.reshape(groups, 8, full), axis=0)
            out_t = out_t + lax.dot_general(
                kv[b, j, 1], p.astype(BF16), CONTRACT_FIRST, preferred_element_type=F32)
        inverse = 1.0 / jnp.sum(total, axis=0, keepdims=True)
        out_t = out_t * inverse
        g_t = g.astype(F32).T
        ob[j] = out_t.T.astype(BF16)
        delta = jnp.sum(out_t.astype(BF16).astype(F32) * g_t, axis=0, keepdims=True)
        dq_t = jnp.zeros((HD, full), F32)
        for b in (0, 2, 1):
            probs = scores[b] * inverse
            dp = lax.dot_general(kv[b, j, 1], g, CONTRACT_LAST, preferred_element_type=F32)
            ds = (probs * (dp - delta)).astype(BF16)
            dk = jnp.dot(ds, q, preferred_element_type=F32) * SCALE
            dv = jnp.dot(probs.astype(BF16), g, preferred_element_type=F32)
            dq_t = dq_t + lax.dot_general(
                kv[b, j, 0], ds, CONTRACT_FIRST, preferred_element_type=F32)
            if b == 1:
                own_grad[j, 0] = dk
                own_grad[j, 1] = dv
            else:
                back_send[1 - b // 2, j, 0] = dk.astype(BF16)
                back_send[1 - b // 2, j, 1] = dv.astype(BF16)
        dqb[j] = (dq_t * SCALE).T.astype(BF16)
        for t in range(2):
            for d in range(2):
                x_back(d, t, j).start()
        for t in range(2):
            z_back(t, j).start()
            store(t, j).start()

    each(head)

    def finish(j):
        for t in range(2):
            for d in range(2):
                x_back(d, t, j).wait_recv()
            grad = own_grad[j, t] + back_recv[0, j, t].astype(F32) + back_recv[1, j, t].astype(F32)
            grad_out[j, t] = grad.astype(BF16)
        for t in range(2, 4):
            z_back(t, j).start()
            store(t, j).start()

    each(finish)

    def drain(j):
        for t in range(4):
            z_forward(t, j).wait_send()
            z_back(t, j).wait_send()
            z_back(t, j).wait_recv()
            store(t, j).wait()
        for d in range(2):
            for t in range(2):
                x_own(d, t, j).wait_send()
                x_peer(d, t, j).wait_send()
                x_back(d, t, j).wait_send()

    each(drain)


def on_device(query_rows, key_rows, value_rows, out_grad, window_offsets):
    frames, lats, lons, width = query_rows.shape
    heads = width // HD // 2
    rows = frames * lats * lons
    full = 2 * rows
    flat = lambda x: x.reshape(rows, width)
    offs = jnp.pad(window_offsets[0], ((0, 6), (0, 126)))
    sem = pltpu.SemaphoreType.DMA
    body = lambda *refs: kernel(heads, rows, lats, lons, *refs)
    outs = pl.pallas_call(
        body,
        out_shape=[jax.ShapeDtypeStruct((rows, width), BF16)] * 4,
        in_specs=[pl.BlockSpec(memory_space=pl.ANY)] * 5,
        out_specs=[pl.BlockSpec(memory_space=pl.ANY)] * 4,
        scratch_shapes=[
            pltpu.VMEM((heads, full, HD), BF16),
            pltpu.VMEM((heads, full, HD), BF16),
            pltpu.VMEM((3, heads, 2, full, HD), BF16),
            pltpu.VMEM((2, 8, 128), jnp.int32),
            pltpu.VMEM((3, 8, full), F32),
            pltpu.VMEM((3, full, full), F32),
            pltpu.VMEM((heads, full, HD), BF16),
            pltpu.VMEM((heads, full, HD), BF16),
            pltpu.VMEM((2, heads, 2, full, HD), BF16),
            pltpu.VMEM((2, heads, 2, full, HD), BF16),
            pltpu.VMEM((heads, 2, full, HD), F32),
            pltpu.VMEM((heads, 2, full, HD), BF16),
            sem((4, heads)),
            sem((3,)),
            sem((4, heads)),
            sem((4, heads)),
            sem((2, 2, heads)),
            sem((2, 2, heads)),
            sem((2, 2, heads)),
            sem((2, 2, heads)),
            sem((2, 2, heads)),
            sem((2, 2, heads)),
            sem((4, heads)),
            sem((4, heads)),
            sem((4, heads)),
        ],
        compiler_params=pltpu.CompilerParams(collective_id=0, has_side_effects=True),
    )(flat(query_rows), flat(key_rows), flat(value_rows), flat(out_grad), offs)
    return tuple(x.reshape(frames, lats, lons, width) for x in outs)


def solution(mesh):
    rows = P("tm", None, "lon", "head")
    return jax.shard_map(
        on_device,
        mesh=mesh,
        in_specs=(rows, rows, rows, rows, P("tm", None, "lon")),
        out_specs=(rows, rows, rows, rows),
        check_vma=False,
    )
```

```python
import math

import jax
import jax.numpy as jnp
from jax import lax
from jax.experimental import pallas as pl
from jax.experimental.pallas import tpu as pltpu
from jax.sharding import PartitionSpec as P

HD = 128
TILE = 4
MESH = pl.DeviceIdType.MESH
SCALE = 1.0 / math.sqrt(HD)
EXP_SCALE = SCALE / math.log(2.0)
FAR = -1e30
BF16 = jnp.bfloat16
F32 = jnp.float32
CONTRACT_LAST = (((1,), (1,)), ((), ()))
CONTRACT_FIRST = (((0,), (0,)), ((), ()))


def kernel(
    heads, rows, lats, lons,
    q_in, k_in, v_in, g_in, off_in,
    o_out, dq_out, dk_out, dv_out,
    qb, gb, kv, offs, bias, scores, ob, dqb, back_send, back_recv, own_grad, grad_out,
    load_sem, off_sem, zf_send, zf_recv, xo_send, xo_recv, xp_send, xp_recv,
    xb_send, xb_recv, zb_send, zb_recv, out_sem,
):
    me = lax.axis_index("tm")
    lon = lax.axis_index("lon")
    count = lax.axis_size("lon")
    peer = 1 - me
    sides = (lax.rem(lon + 1, count), lax.rem(lon + count - 1, count))
    full = 2 * rows
    args = (k_in, v_in, q_in, g_in)
    outs = (o_out, dq_out, dk_out, dv_out)

    def columns(owner, j):
        return pl.ds(pl.multiple_of((owner * heads + j) * HD, HD), HD)

    def half(owner):
        return pl.ds(pl.multiple_of(owner * rows, rows), rows)

    def slot(t, j):
        part = kv.at[1, j, t] if t < 2 else (qb.at[j] if t == 2 else gb.at[j])
        return part.at[half(me)]

    def load(t, j):
        return pltpu.make_async_copy(args[t].at[:, columns(me, j)], slot(t, j), load_sem.at[t, j])

    def z_forward(t, j):
        return pltpu.make_async_remote_copy(
            args[t].at[:, columns(peer, j)], slot(t, j), zf_send.at[t, j], zf_recv.at[t, j],
            device_id={"tm": peer}, device_id_type=MESH)

    def x_own(d, t, j):
        return pltpu.make_async_remote_copy(
            args[t].at[:, columns(me, j)], kv.at[2 * d, j, t, half(me)],
            xo_send.at[d, t, j], xo_recv.at[d, t, j],
            device_id={"lon": sides[d]}, device_id_type=MESH)

    def x_peer(d, t, j):
        return pltpu.make_async_remote_copy(
            kv.at[1, j, t, half(peer)], kv.at[2 * d, j, t, half(peer)],
            xp_send.at[d, t, j], xp_recv.at[d, t, j],
            device_id={"lon": sides[d]}, device_id_type=MESH)

    def x_back(h, d, t, j):
        part = half((peer, me)[h])
        return pltpu.make_async_remote_copy(
            back_send.at[d, j, t, part], back_recv.at[d, j, t, part],
            xb_send.at[h, d, t, j], xb_recv.at[h, d, t, j],
            device_id={"lon": sides[d]}, device_id_type=MESH)

    def result(t, j):
        return (ob.at[j], dqb.at[j], grad_out.at[j, 0], grad_out.at[j, 1])[t]

    def z_back(t, j):
        return pltpu.make_async_remote_copy(
            result(t, j).at[half(peer)], outs[t].at[:, columns(me, j)],
            zb_send.at[t, j], zb_recv.at[t, j],
            device_id={"tm": peer}, device_id_type=MESH)

    def store(t, j):
        return pltpu.make_async_copy(
            result(t, j).at[half(me)], outs[t].at[:, columns(me, j)], out_sem.at[t, j])

    off_load = pltpu.make_async_copy(off_in.at[0], offs.at[me], off_sem.at[0])
    off_send = pltpu.make_async_remote_copy(
        off_in.at[0], offs.at[me], off_sem.at[1], off_sem.at[2],
        device_id={"tm": peer}, device_id_type=MESH)

    def each(body):
        lax.fori_loop(0, heads, lambda j, c: (body(j), c)[1], 0)

    barrier = pltpu.get_barrier_semaphore()
    pl.semaphore_signal(barrier, inc=1, device_id={"tm": peer}, device_id_type=MESH)
    for side in sides:
        pl.semaphore_signal(barrier, inc=1, device_id={"lon": side}, device_id_type=MESH)
    pl.semaphore_wait(barrier, 3)

    off_send.start()
    off_load.start()

    def begin(j):
        for t in range(2):
            z_forward(t, j).start()
            for d in range(2):
                x_own(d, t, j).start()
        for t in range(4):
            load(t, j).start()

    each(begin)

    def begin_queries(j):
        for t in range(2, 4):
            z_forward(t, j).start()

    each(begin_queries)

    off_load.wait()
    off_send.wait()
    query = lax.broadcasted_iota(jnp.int32, (8, full), 1)
    sub = lax.broadcasted_iota(jnp.int32, (8, full), 0)
    q_frame = query // rows
    q_lat = (query // (lons * TILE)) % 2
    q_lon = (query // TILE) % 2
    centre = q_lon
    for f in range(2):
        for a in range(2):
            for b in range(2):
                value = offs[f, a : a + 1, b : b + 1]
                hit = (q_frame == f) & (q_lat == a) & (q_lon == b)
                centre = centre + jnp.where(hit, value, 0)
    for b in range(3):
        gap = sub // TILE + (2 * b - 2) - centre
        bias[b] = jnp.where(jnp.abs(gap) <= 1, 0.0, FAR).astype(F32)

    def forward_peer(j):
        for t in range(2):
            z_forward(t, j).wait_recv()
            for d in range(2):
                x_peer(d, t, j).start()

    each(forward_peer)

    groups = full // 8

    def head(j):
        for t in range(4):
            load(t, j).wait()
        for t in range(2, 4):
            z_forward(t, j).wait_recv()
        for d in range(2):
            for t in range(2):
                x_own(d, t, j).wait_recv()
                x_peer(d, t, j).wait_recv()
        q = qb[j]
        g = gb[j]
        peak = None
        for b in range(3):
            s = lax.dot_general(kv[b, j, 0], q, CONTRACT_LAST, preferred_element_type=F32)
            s = s.reshape(groups, 8, full) + bias[b]
            scores[b] = s.reshape(full, full)
            top = jnp.max(s, axis=0)
            peak = top if peak is None else jnp.maximum(peak, top)
        peak = jnp.max(peak, axis=0, keepdims=True)
        total = jnp.zeros((8, full), F32)
        out_t = jnp.zeros((HD, full), F32)
        for b in range(3):
            p = jnp.exp2((scores[b] - peak) * EXP_SCALE)
            scores[b] = p
            total = total + jnp.sum(p.reshape(groups, 8, full), axis=0)
            out_t = out_t + lax.dot_general(
                kv[b, j, 1], p.astype(BF16), CONTRACT_FIRST, preferred_element_type=F32)
        inverse = 1.0 / jnp.sum(total, axis=0, keepdims=True)
        out_t = out_t * inverse
        g_t = g.astype(F32).T
        ob[j] = out_t.T.astype(BF16)
        delta = jnp.sum(out_t.astype(BF16).astype(F32) * g_t, axis=0, keepdims=True)
        dq_t = jnp.zeros((HD, full), F32)
        for b in (0, 2, 1):
            probs = scores[b] * inverse
            dp = lax.dot_general(kv[b, j, 1], g, CONTRACT_LAST, preferred_element_type=F32)
            ds = (probs * (dp - delta)).astype(BF16)
            dk = jnp.dot(ds, q, preferred_element_type=F32) * SCALE
            dv = jnp.dot(probs.astype(BF16), g, preferred_element_type=F32)
            dq_t = dq_t + lax.dot_general(
                kv[b, j, 0], ds, CONTRACT_FIRST, preferred_element_type=F32)
            if b == 1:
                own_grad[j, 0] = dk
                own_grad[j, 1] = dv
            else:
                back_send[1 - b // 2, j, 0] = dk.astype(BF16)
                back_send[1 - b // 2, j, 1] = dv.astype(BF16)
        dqb[j] = (dq_t * SCALE).T.astype(BF16)
        for t in range(2):
            for d in range(2):
                x_back(0, d, t, j).start()
        for t in range(2):
            z_back(t, j).start()
            store(t, j).start()

    each(head)

    def return_own(j):
        for t in range(2):
            for d in range(2):
                x_back(1, d, t, j).start()

    each(return_own)

    def add_up(h, j):
        part = half((peer, me)[h])
        for t in range(2):
            for d in range(2):
                x_back(h, d, t, j).wait_recv()
            grad = own_grad[j, t, part]
            for d in range(2):
                grad = grad + back_recv[d, j, t, part].astype(F32)
            grad_out[j, t, part] = grad.astype(BF16)

    def finish_peer(j):
        add_up(0, j)
        for t in range(2, 4):
            z_back(t, j).start()

    each(finish_peer)

    def finish_own(j):
        add_up(1, j)
        for t in range(2, 4):
            store(t, j).start()

    each(finish_own)

    def drain(j):
        for t in range(4):
            z_forward(t, j).wait_send()
            z_back(t, j).wait_send()
            z_back(t, j).wait_recv()
            store(t, j).wait()
        for d in range(2):
            for t in range(2):
                x_own(d, t, j).wait_send()
                x_peer(d, t, j).wait_send()
                for h in range(2):
                    x_back(h, d, t, j).wait_send()

    each(drain)


def move(*refs):
    count = len(refs) // 2
    sems = refs[-1]
    copies = [pltpu.make_async_copy(refs[i], refs[count + i], sems.at[i]) for i in range(4)]
    for copy in copies:
        copy.start()
    for copy in copies:
        copy.wait()


def on_device(query_rows, key_rows, value_rows, out_grad, window_offsets):
    frames, lats, lons, width = query_rows.shape
    heads = width // HD // 2
    rows = frames * lats * lons
    full = 2 * rows
    flat = lambda x: x.reshape(rows, width)
    sem = pltpu.SemaphoreType.DMA
    body = lambda *refs: kernel(heads, rows, lats, lons, *refs)
    outs = pl.pallas_call(
        body,
        out_shape=[pltpu.VMEM((rows, width), BF16)] * 4,
        in_specs=[pl.BlockSpec(memory_space=pl.ANY)] * 5,
        out_specs=[pl.BlockSpec(memory_space=pl.ANY)] * 4,
        scratch_shapes=[
            pltpu.VMEM((heads, full, HD), BF16),
            pltpu.VMEM((heads, full, HD), BF16),
            pltpu.VMEM((3, heads, 2, full, HD), BF16),
            pltpu.VMEM((2, 2, 2), jnp.int32),
            pltpu.VMEM((3, 8, full), F32),
            pltpu.VMEM((3, full, full), F32),
            pltpu.VMEM((heads, full, HD), BF16),
            pltpu.VMEM((heads, full, HD), BF16),
            pltpu.VMEM((2, heads, 2, full, HD), BF16),
            pltpu.VMEM((2, heads, 2, full, HD), BF16),
            pltpu.VMEM((heads, 2, full, HD), F32),
            pltpu.VMEM((heads, 2, full, HD), BF16),
            sem((4, heads)),
            sem((3,)),
            sem((4, heads)),
            sem((4, heads)),
            sem((2, 2, heads)),
            sem((2, 2, heads)),
            sem((2, 2, heads)),
            sem((2, 2, heads)),
            sem((2, 2, 2, heads)),
            sem((2, 2, 2, heads)),
            sem((4, heads)),
            sem((4, heads)),
            sem((4, heads)),
        ],
        compiler_params=pltpu.CompilerParams(collective_id=0, has_side_effects=True),
    )(flat(query_rows), flat(key_rows), flat(value_rows), flat(out_grad), window_offsets)
    outs = pl.pallas_call(
        move,
        out_shape=[jax.ShapeDtypeStruct((rows, width), BF16)] * 4,
        in_specs=[pl.BlockSpec(memory_space=pl.ANY)] * 4,
        out_specs=[pl.BlockSpec(memory_space=pl.ANY)] * 4,
        scratch_shapes=[sem((4,))],
        compiler_params=pltpu.CompilerParams(vmem_limit_bytes=1 << 20),
    )(*outs)
    return tuple(x.reshape(frames, lats, lons, width) for x in outs)


def solution(mesh):
    rows = P("tm", None, "lon", "head")
    return jax.shard_map(
        on_device,
        mesh=mesh,
        in_specs=(rows, rows, rows, rows, P("tm", None, "lon")),
        out_specs=(rows, rows, rows, rows),
        check_vma=False,
    )
```

```python
import math

import jax
import jax.numpy as jnp
from jax import lax
from jax.experimental import pallas as pl
from jax.experimental.pallas import tpu as pltpu
from jax.sharding import PartitionSpec as P

HD = 128
TILE = 4
MESH = pl.DeviceIdType.MESH
SCALE = 1.0 / math.sqrt(HD)
EXP_SCALE = SCALE / math.log(2.0)
FAR = -1e30
BF16 = jnp.bfloat16
F32 = jnp.float32
CONTRACT_LAST = (((1,), (1,)), ((), ()))
CONTRACT_FIRST = (((0,), (0,)), ((), ()))


def kernel(
    heads, rows, lats, lons,
    q_in, k_in, v_in, g_in, off_in,
    out,
    qg, kv, offs, bias, scores, result, back_send, back_recv, own_grad,
    load_sem, off_sem, zf_send, zf_recv, xo_send, xo_recv, xf_send, xf_recv, xb_send, xb_recv,
    zb_send, zb_recv, out_sem,
):
    me = lax.axis_index("tm")
    lon = lax.axis_index("lon")
    count = lax.axis_size("lon")
    peer = 1 - me
    sides = (lax.rem(lon + 1, count), lax.rem(lon + count - 1, count))
    full = 2 * rows
    args = (k_in, v_in, q_in, g_in)

    def columns(owner, j):
        return pl.ds(pl.multiple_of((owner * heads + j) * HD, HD), HD)

    def half(owner):
        return pl.ds(pl.multiple_of(owner * rows, rows), rows)

    def slot(t, j):
        place = kv.at[1, j, t] if t < 2 else qg.at[j, t - 2]
        return place.at[half(me)]

    def load(t, j):
        return pltpu.make_async_copy(args[t].at[:, columns(me, j)], slot(t, j), load_sem.at[t, j])

    def z_forward(t, j):
        return pltpu.make_async_remote_copy(
            args[t].at[:, columns(peer, j)], slot(t, j), zf_send.at[t, j], zf_recv.at[t, j],
            device_id={"tm": peer}, device_id_type=MESH)

    def x_own(d):
        return pltpu.make_async_remote_copy(
            kv.at[1, :, :, half(me)], kv.at[2 * d, :, :, half(me)],
            xo_send.at[d], xo_recv.at[d],
            device_id={"lon": sides[d]}, device_id_type=MESH)

    def x_peer(d, j):
        return pltpu.make_async_remote_copy(
            kv.at[1, j, :, half(peer)], kv.at[2 * d, j, :, half(peer)],
            xf_send.at[d, j], xf_recv.at[d, j],
            device_id={"lon": sides[d]}, device_id_type=MESH)

    def x_back(h, d, j):
        return pltpu.make_async_remote_copy(
            back_send.at[d, j, :, half((peer, me)[h])], back_recv.at[h, d, j],
            xb_send.at[h, d, j], xb_recv.at[h, d, j],
            device_id={"lon": sides[d]}, device_id_type=MESH)

    def z_back(pair, j):
        return pltpu.make_async_remote_copy(
            result.at[j, pl.ds(2 * pair, 2), half(peer)],
            out.at[pl.ds(2 * pair, 2), :, columns(me, j)],
            zb_send.at[pair, j], zb_recv.at[pair, j],
            device_id={"tm": peer}, device_id_type=MESH)

    def store(j):
        return pltpu.make_async_copy(
            result.at[j, pl.ds(0, 2), half(me)],
            out.at[pl.ds(0, 2), :, columns(me, j)], out_sem.at[j])

    off_load = pltpu.make_async_copy(off_in.at[0], offs.at[me], off_sem.at[0])
    off_send = pltpu.make_async_remote_copy(
        off_in.at[0], offs.at[me], off_sem.at[1], off_sem.at[2],
        device_id={"tm": peer}, device_id_type=MESH)

    def each(body):
        lax.fori_loop(0, heads, lambda j, c: (body(j), c)[1], 0)

    barrier = pltpu.get_barrier_semaphore()
    pl.semaphore_signal(barrier, inc=1, device_id={"tm": peer}, device_id_type=MESH)
    for side in sides:
        pl.semaphore_signal(barrier, inc=1, device_id={"lon": side}, device_id_type=MESH)


    def begin(j):
        for t in range(2):
            load(t, j).start()

    def begin_keys(j):
        for t in range(2):
            z_forward(t, j).start()

    def begin_queries(j):
        for t in range(2, 4):
            z_forward(t, j).start()
            load(t, j).start()

    def wait_keys(j):
        for t in range(2):
            load(t, j).wait()

    each(begin)
    pl.semaphore_wait(barrier, 3)
    each(begin_keys)
    each(wait_keys)
    for d in range(2):
        x_own(d).start()
    off_send.start()
    off_load.start()
    each(begin_queries)
    off_load.wait()
    off_send.wait()
    query = lax.broadcasted_iota(jnp.int32, (8, full), 1)
    sub = lax.broadcasted_iota(jnp.int32, (8, full), 0)
    q_frame = query // rows
    q_lat = (query // (lons * TILE)) % 2
    q_lon = (query // TILE) % 2
    centre = q_lon
    for f in range(2):
        for a in range(2):
            for b in range(2):
                value = offs[f, a : a + 1, b : b + 1]
                hit = (q_frame == f) & (q_lat == a) & (q_lon == b)
                centre = centre + jnp.where(hit, value, 0)
    for b in range(3):
        gap = sub // TILE + (2 * b - 2) - centre
        bias[b] = jnp.where(jnp.abs(gap) <= 1, 0.0, FAR).astype(F32)

    def forward_peer(j):
        for t in range(2):
            z_forward(t, j).wait_recv()
        for d in range(2):
            x_peer(d, j).start()

    each(forward_peer)

    groups = full // 8
    for d in range(2):
        x_own(d).wait_recv()

    def head(j):
        for t in range(2, 4):
            load(t, j).wait()
            z_forward(t, j).wait_recv()
        for d in range(2):
            x_peer(d, j).wait_recv()
        q = qg[j, 0]
        g = qg[j, 1]
        peak = None
        for b in range(3):
            s = lax.dot_general(kv[b, j, 0], q, CONTRACT_LAST, preferred_element_type=F32)
            s = s.reshape(groups, 8, full) + bias[b]
            scores[b] = s.reshape(full, full)
            top = jnp.max(s, axis=0)
            peak = top if peak is None else jnp.maximum(peak, top)
        peak = jnp.max(peak, axis=0, keepdims=True)
        total = jnp.zeros((8, full), F32)
        out_t = jnp.zeros((HD, full), F32)
        for b in range(3):
            p = jnp.exp2((scores[b] - peak) * EXP_SCALE)
            scores[b] = p
            total = total + jnp.sum(p.reshape(groups, 8, full), axis=0)
            out_t = out_t + lax.dot_general(
                kv[b, j, 1], p.astype(BF16), CONTRACT_FIRST, preferred_element_type=F32)
        inverse = 1.0 / jnp.sum(total, axis=0, keepdims=True)
        out_t = out_t * inverse
        g_t = g.astype(F32).T
        result[j, 0] = out_t.T.astype(BF16)
        delta = jnp.sum(out_t.astype(BF16).astype(F32) * g_t, axis=0, keepdims=True)
        dq_t = jnp.zeros((HD, full), F32)
        for b in (0, 2, 1):
            probs = scores[b] * inverse
            dp = lax.dot_general(kv[b, j, 1], g, CONTRACT_LAST, preferred_element_type=F32)
            ds = (probs * (dp - delta)).astype(BF16)
            dk = jnp.dot(ds, q, preferred_element_type=F32) * SCALE
            dv = jnp.dot(probs.astype(BF16), g, preferred_element_type=F32)
            dq_t = dq_t + lax.dot_general(
                kv[b, j, 0], ds, CONTRACT_FIRST, preferred_element_type=F32)
            if b == 1:
                own_grad[j, 0] = dk
                own_grad[j, 1] = dv
            else:
                back_send[1 - b // 2, j, 0] = dk.astype(BF16)
                back_send[1 - b // 2, j, 1] = dv.astype(BF16)
        result[j, 1] = (dq_t * SCALE).T.astype(BF16)
        for d in range(2):
            x_back(0, d, j).start()
        z_back(0, j).start()
        store(j).start()

    each(head)

    def return_own(j):
        for d in range(2):
            x_back(1, d, j).start()

    each(return_own)

    def add_up(h, j, t):
        grad = own_grad[j, t, half((peer, me)[h])]
        for d in range(2):
            grad = grad + back_recv[h, d, j, t].astype(F32)
        return grad.astype(BF16)

    def finish_peer(j):
        for d in range(2):
            x_back(0, d, j).wait_recv()
        for t in range(2):
            result[j, 2 + t, half(peer)] = add_up(0, j, t)
        z_back(1, j).start()

    each(finish_peer)

    def finish_own(j):
        for d in range(2):
            x_back(1, d, j).wait_recv()
        for t in range(2):
            out[2 + t, :, columns(me, j)] = add_up(1, j, t)

    each(finish_own)

    for d in range(2):
        x_own(d).wait_send()

    def drain(j):
        for t in range(4):
            z_forward(t, j).wait_send()
        for pair in range(2):
            z_back(pair, j).wait_send()
            z_back(pair, j).wait_recv()
        store(j).wait()
        for d in range(2):
            x_peer(d, j).wait_send()
            for h in range(2):
                x_back(h, d, j).wait_send()

    each(drain)


def move(packed, *refs):
    outs, sems = refs[:-1], refs[-1]
    copies = [
        pltpu.make_async_copy(packed.at[i], out, sems.at[i]) for i, out in enumerate(outs)
    ]
    for copy in copies:
        copy.start()
    for copy in copies:
        copy.wait()


def on_device(query_rows, key_rows, value_rows, out_grad, window_offsets):
    frames, lats, lons, width = query_rows.shape
    heads = width // HD // 2
    rows = frames * lats * lons
    full = 2 * rows
    flat = lambda x: x.reshape(rows, width)
    sem = pltpu.SemaphoreType.DMA
    body = lambda *refs: kernel(heads, rows, lats, lons, *refs)
    packed = pl.pallas_call(
        body,
        out_shape=pltpu.VMEM((4, rows, width), BF16),
        in_specs=[pl.BlockSpec(memory_space=pl.ANY)] * 5,
        out_specs=pl.BlockSpec(memory_space=pltpu.VMEM),
        scratch_shapes=[
            pltpu.VMEM((heads, 2, full, HD), BF16),
            pltpu.VMEM((3, heads, 2, full, HD), BF16),
            pltpu.VMEM((2, 2, 2), jnp.int32),
            pltpu.VMEM((3, 8, full), F32),
            pltpu.VMEM((3, full, full), F32),
            pltpu.VMEM((heads, 4, full, HD), BF16),
            pltpu.VMEM((2, heads, 2, full, HD), BF16),
            pltpu.VMEM((2, 2, heads, 2, rows, HD), BF16),
            pltpu.VMEM((heads, 2, full, HD), F32),
            sem((4, heads)),
            sem((3,)),
            sem((4, heads)),
            sem((4, heads)),
            sem((2,)),
            sem((2,)),
            sem((2, heads)),
            sem((2, heads)),
            sem((2, 2, heads)),
            sem((2, 2, heads)),
            sem((2, heads)),
            sem((2, heads)),
            sem((heads,)),
        ],
        compiler_params=pltpu.CompilerParams(collective_id=0, has_side_effects=True),
    )(flat(query_rows), flat(key_rows), flat(value_rows), flat(out_grad), window_offsets)
    outs = pl.pallas_call(
        move,
        out_shape=[jax.ShapeDtypeStruct((rows, width), BF16)] * 4,
        in_specs=[pl.BlockSpec(memory_space=pl.ANY)],
        out_specs=[pl.BlockSpec(memory_space=pl.ANY)] * 4,
        scratch_shapes=[sem((4,))],
        compiler_params=pltpu.CompilerParams(vmem_limit_bytes=1 << 20),
    )(packed)
    return tuple(x.reshape(frames, lats, lons, width) for x in outs)


def solution(mesh):
    rows = P("tm", None, "lon", "head")
    return jax.shard_map(
        on_device,
        mesh=mesh,
        in_specs=(rows, rows, rows, rows, P("tm", None, "lon")),
        out_specs=(rows, rows, rows, rows),
        check_vma=False,
    )
```
